32 devices in a mesh: dp: 8 (over y, x, core), seq: 4 (over z).
Axes of the slice: x: 2, y: 2, z: 4, core: 2. Of those that a mesh axis runs over, the one named last changes fastest.
Arguments:
- queries: bfloat16 [8192, 8192], P(('dp', 'seq')), may hold values from -60 to 60
- keys: bfloat16 [8192, 1024], P(('dp', 'seq')), may hold values from -60 to 60
- values: bfloat16 [8192, 1024], P(('dp', 'seq')), may hold values from -6 to 6
- plan: int32 [8192], P(('dp', 'seq')), may hold values from 0 to 8191, as said below
- segment_ids: int32 [8192], P(('dp', 'seq')), may hold values from 0 to 63, as said below
Outputs:
- attended: bfloat16 [8192, 8192], P(('dp', 'seq'))
The draws below stay inside these ranges and needn't reach their ends.
Inputs may be any that keep to these rules, and one draw needn't show every extreme that they name: `plan`: A permutation of the owner rows. The rows of one device go exactly 8 to each device (owner rows d * 256 to (d + 1) * 256 - 1 belong to device d), in random order among the device's rows. `segment_ids`: documents are runs of equal ids that never fall; every length is a multiple of 128; no document crosses a boundary of the aligned blocks of 1024 owner rows; one document fills a whole block.
All inputs are finite; a program needn't handle non-finite values.
Results may differ from the reference program's by a relative error of at most 0.0053.
Values may be sent and summed in bfloat16 or wider, within the bound.
A program may use at most 128 MiB of HBM per device.

```python
import jax
import jax.numpy as jnp
from jax import lax

H = 64
KVH = 8
HD = 128
TOK_DEV = 256
TOKENS = 8192
GROUP = 1024


def make_plan(key):
    devices = TOKENS // TOK_DEV
    share = TOK_DEV // devices
    alpha = jax.random.permutation(jax.random.fold_in(key, 101), devices).astype(jnp.int32)
    beta = jax.random.permutation(jax.random.fold_in(key, 102), devices).astype(jnp.int32)
    gamma = jax.random.permutation(jax.random.fold_in(key, 103), devices).astype(jnp.int32)
    slots = jnp.arange(TOK_DEV, dtype=jnp.int32)
    blocks = slots // share
    target = alpha[(beta[:, None] + gamma[blocks][None, :]) % devices]
    owner_rows = target * TOK_DEV + slots[None, :]
    shuffle_keys = jax.random.split(jax.random.fold_in(key, 104), devices)
    shuffles = jax.vmap(lambda single: jax.random.permutation(single, TOK_DEV))(shuffle_keys).astype(jnp.int32)
    placed = jnp.take_along_axis(owner_rows, shuffles, axis=1)
    return placed.reshape(TOKENS).astype(jnp.int32)


def draw_plan(key, part):
    return make_plan(key)


def draw_segment_ids(key, part):
    unit = TOK_DEV // 2
    units = TOKENS // unit
    per_group = GROUP // unit
    groups = units // per_group
    places = jnp.arange(units, dtype=jnp.int32)
    inside = places % per_group
    rolls = jax.random.randint(jax.random.fold_in(key, 201), (units,), 0, 20).astype(jnp.int32)
    limit = jnp.where(inside % 2 == 1, 3, 9)
    cuts = jnp.where(rolls < limit, 1, 0).astype(jnp.int32)
    whole = jax.random.randint(jax.random.fold_in(key, 202), (), 0, groups).astype(jnp.int32)
    cuts = jnp.where(places // per_group == whole, 0, cuts)
    cuts = jnp.where(inside == 0, 1, cuts)
    cuts = jnp.where(places == units - 1, 1, cuts)
    labels = lax.cummax(jnp.where(cuts == 1, places, jnp.zeros_like(places)), axis=0)
    return jnp.repeat(labels, unit).astype(jnp.int32)


def draw_queries(key, part):
    base = jnp.clip(jax.random.normal(jax.random.fold_in(key, 402), (TOKENS, H * HD), jnp.float32), -6.0, 6.0)
    return base.astype(jnp.bfloat16)


def draw_keys(key, part):
    base = jnp.clip(jax.random.normal(jax.random.fold_in(key, 502), (TOKENS, KVH * HD), jnp.float32), -6.0, 6.0)
    return base.astype(jnp.bfloat16)


def block_levels(stream_key, extent, cuts, low, top_value):
    def one(position, parts):
        heights = jax.random.uniform(jax.random.fold_in(jax.random.fold_in(stream_key, 6), position), (parts,), jnp.float32, low / len(cuts), top_value / len(cuts))
        return jnp.repeat(jnp.exp(heights), extent[position] // parts).reshape((-1,) + (1,) * (len(extent) - position - 1))

    loudness = one(*cuts[0])
    for cut in cuts[1:]:
        loudness = loudness * one(*cut)
    return loudness


def scatter_about(stream_key, dims, deviation, most, cuts=(), kind=jnp.bfloat16):
    values = jax.random.normal(stream_key, dims, jnp.float32) * deviation
    if len(cuts) > 0:
        values = block_levels(stream_key, dims, cuts, -0.22, 0.18) * values
    return jnp.clip(values, min=-most, max=most).astype(kind)


def setup_inputs(seed: int = 0) -> dict:
    key_of = jax.random.split(jax.random.key(seed), 6)
    return {
        "queries": draw_queries(jax.random.fold_in(key_of[5], 71), 0),
        "keys": draw_keys(jax.random.fold_in(key_of[5], 71), 0),
        "values": scatter_about(key_of[2], (TOKENS, KVH * HD), 1.0, 6.0, ((0, 32),)),
        "plan": draw_plan(jax.random.fold_in(key_of[5], 71), 0),
        "segment_ids": draw_segment_ids(jax.random.fold_in(key_of[5], 71), 0),
    }


theta_base = 500000.0
tile_rows = 512


def doc_positions(segment_ids):
    places = jnp.arange(segment_ids.shape[0], dtype=jnp.int32)
    starts = jnp.concatenate([jnp.ones((1,), jnp.bool_), segment_ids[1:] != segment_ids[:-1]])
    first = lax.cummax(jnp.where(starts, places, jnp.zeros_like(places)), axis=0)
    return places - first


def rotate(source, positions):
    width = source.shape[-1]
    half = width // 2
    freqs = theta_base ** (-2.0 * jnp.arange(half, dtype=jnp.float32) / width)
    angles = positions.astype(jnp.float32)[:, None] * freqs[None, :]
    cosine = jnp.cos(angles)[:, None, :]
    sine = jnp.sin(angles)[:, None, :]
    floats = source.astype(jnp.float32)
    lower = floats[..., :half]
    upper = floats[..., half:]
    turned = jnp.concatenate([lower * cosine - upper * sine, upper * cosine + lower * sine], axis=-1)
    return turned.astype(jnp.bfloat16)


def masked_block(query_block, key_part, value_part, query_ids, key_ids, anchor):
    count = query_block.shape[0]
    reach = key_part.shape[0]
    scores = jnp.einsum("qkgd,tkd->kgqt", query_block.astype(jnp.float32), key_part.astype(jnp.float32)) * (HD ** -0.5)
    query_rows = anchor + jnp.arange(count, dtype=jnp.int32)
    key_rows = jnp.arange(reach, dtype=jnp.int32)
    allowed = (key_rows[None, :] <= query_rows[:, None]) & (key_ids[None, :] == query_ids[:, None])
    scores = jnp.where(allowed, scores, -jnp.inf)
    peak = jnp.max(scores, axis=-1, keepdims=True)
    weights = jnp.exp(scores - peak)
    totals = jnp.sum(weights, axis=-1)
    rounded = lax.optimization_barrier(weights.astype(jnp.bfloat16)).astype(jnp.float32)
    mixed = jnp.einsum("kgqt,tkd->kgqd", rounded, value_part.astype(jnp.float32))
    result = mixed / totals[..., None]
    return jnp.transpose(result, (2, 0, 1, 3)).astype(jnp.bfloat16)


def reference(queries, keys, values, plan, segment_ids):
    total = queries.shape[0]
    per_kv = H // KVH
    own_q = jnp.zeros_like(queries).at[plan].set(queries)
    own_k = jnp.zeros_like(keys).at[plan].set(keys)
    own_v = jnp.zeros_like(values).at[plan].set(values)
    positions = doc_positions(segment_ids)
    rot_q = rotate(own_q.reshape(total, H, HD), positions).reshape(total, KVH, per_kv, HD)
    rot_k = rotate(own_k.reshape(total, KVH, HD), positions)
    own_v = own_v.reshape(total, KVH, HD)

    def one_group(number):
        start = number * GROUP
        group_q = lax.dynamic_slice_in_dim(rot_q, start, GROUP, 0)
        group_k = lax.dynamic_slice_in_dim(rot_k, start, GROUP, 0)
        group_v = lax.dynamic_slice_in_dim(own_v, start, GROUP, 0)
        group_ids = lax.dynamic_slice_in_dim(segment_ids, start, GROUP, 0)
        pieces = []
        for block in range(GROUP // tile_rows):
            low = block * tile_rows
            high = low + tile_rows
            pieces.append(masked_block(group_q[low:high], group_k[:high], group_v[:high], group_ids[low:high], group_ids[:high], low))
        return jnp.concatenate(pieces, axis=0)

    outputs = lax.map(one_group, jnp.arange(total // GROUP, dtype=jnp.int32))
    own_out = outputs.reshape(total, H * HD)
    return own_out[plan]
```

```python
import functools

import jax
import jax.numpy as jnp
from jax import lax
from jax.experimental import pallas as pl
from jax.experimental.pallas import tpu as pltpu
from jax.sharding import PartitionSpec as P

H = 64
KVH = 8
HD = 128
theta_base = 500000.0
UNIT = 128
META = 128
LOG2E = 1.4426950408889634


def onehot_rows(index, count):
    return (index[None, :] == jnp.arange(count, dtype=jnp.int32)[:, None]).astype(jnp.bfloat16)


def permuted(onehot, rows):
    return jnp.dot(onehot, rows, preferred_element_type=jnp.float32).astype(jnp.bfloat16)


def turns(positions):
    half = HD // 2
    freqs = theta_base ** (-2.0 * jnp.arange(half, dtype=jnp.float32) / HD)
    angles = positions.astype(jnp.float32)[:, None] * freqs[None, :]
    cosine, sine = jnp.cos(angles), jnp.sin(angles)
    return (
        jnp.concatenate([cosine, cosine], axis=-1),
        jnp.concatenate([-sine, sine], axis=-1),
    )


def attend(seqs, dps, q_ref, k_ref, v_ref, cq, sq, ck, sk, bias, o_ref, ks, vs, ob):
    rows = q_ref.shape[0]
    chunk = rows // seqs
    share = chunk // dps
    per_kv = q_ref.shape[1] // HD

    def arrival(s):
        inner = s % chunk
        return (inner // share) * (seqs * share) + (s // chunk) * share + inner % share

    row = lax.broadcasted_iota(jnp.int32, (rows, rows), 0)
    col = lax.broadcasted_iota(jnp.int32, (rows, rows), 1)
    sort = jnp.where(col == arrival(row), 1.0, 0.0).astype(jnp.bfloat16)
    unsort = jnp.where(row == arrival(col), 1.0, 0.0).astype(jnp.bfloat16)

    def dot(a, b):
        return jnp.dot(a, b, preferred_element_type=jnp.float32)

    def turn(x, c, s):
        return (x * c + pltpu.roll(x, HD // 2, 1) * s).astype(jnp.bfloat16)

    for p in range(seqs):
        part = turn(dot(sort, k_ref[p]), ck[p], sk[p])
        part_v = dot(sort, v_ref[p]).astype(jnp.bfloat16)
        for z in range(seqs):
            ks[z * rows + p * chunk : z * rows + (p + 1) * chunk] = part[z * chunk : (z + 1) * chunk]
            vs[z * rows + p * chunk : z * rows + (p + 1) * chunk] = part_v[z * chunk : (z + 1) * chunk]
    turned = []
    for g in range(per_kv):
        x = dot(sort, q_ref[:, g * HD : (g + 1) * HD])
        turned.append(turn(x, cq[...], sq[...]))
    for c in range(seqs):
        reach = (c + 1) * rows
        block = jnp.concatenate([t[c * chunk : (c + 1) * chunk] for t in turned], axis=0)
        s = lax.dot_general(
            block, ks[:reach], (((1,), (1,)), ((), ())), preferred_element_type=jnp.float32
        )
        s = s.reshape(per_kv, chunk, reach) * (HD ** -0.5 * LOG2E)
        s = s + bias[c * chunk : (c + 1) * chunk, :reach][None]
        e = jnp.exp2(s - jnp.max(s, axis=-1, keepdims=True))
        total = jnp.sum(e, axis=-1, keepdims=True).reshape(per_kv * chunk, 1)
        mixed = dot(e.astype(jnp.bfloat16).reshape(per_kv * chunk, reach), vs[:reach]) / total
        mixed = mixed.astype(jnp.bfloat16)
        for g in range(per_kv):
            ob[c * chunk : (c + 1) * chunk, g * HD : (g + 1) * HD] = mixed[g * chunk : (g + 1) * chunk]
    o_ref[...] = dot(unsort, ob[...]).astype(jnp.bfloat16)


def per_device(queries, keys, values, plan, segment_ids):
    rows = queries.shape[0]
    seqs = lax.axis_size("seq")
    dps = lax.axis_size("dp")
    group = rows * seqs
    share = rows // (seqs * dps)
    chunk = rows // seqs
    per_kv = H // KVH
    unit_ids = lax.all_gather(segment_ids[::UNIT], "seq", axis=0, tiled=True)
    units = unit_ids.shape[0]
    target = plan // rows
    places = jnp.arange(rows, dtype=jnp.int32)
    same = (target[:, None] == target[None, :]) & (places[None, :] < places[:, None])
    slot = target * share + jnp.sum(same.astype(jnp.int32), axis=1)
    onehot = onehot_rows(slot, rows)
    spot = plan % group
    lane = jnp.arange(META, dtype=jnp.int32)[None, :]
    meta = jnp.where(lane == 0, (spot // 32)[:, None], jnp.where(lane == 1, (spot % 32)[:, None], 0))
    kv = jnp.concatenate([keys, values, meta.astype(jnp.bfloat16)], axis=1)

    def swap(x):
        wide = x.shape[-1]
        return lax.all_to_all(
            x.reshape(dps, rows // dps, wide), "dp", split_axis=0, concat_axis=0, tiled=True
        ).reshape(rows, wide)

    kv_here = swap(permuted(onehot, kv))
    q_here = swap(permuted(onehot, queries))
    kv_all = lax.all_gather(kv_here, "seq", axis=0)
    marks = kv_all[:, :, 2 * KVH * HD : 2 * KVH * HD + 2].astype(jnp.int32)
    key_spot = (marks[..., 0] * 32 + marks[..., 1]).reshape(seqs, dps, seqs, share)
    key_spot = key_spot.transpose(0, 2, 1, 3).reshape(seqs, rows)
    mine = lax.axis_index("seq")
    marks = kv_here[:, 2 * KVH * HD : 2 * KVH * HD + 2].astype(jnp.int32)
    q_spot = (marks[..., 0] * 32 + marks[..., 1]).reshape(dps, seqs, share)
    q_spot = q_spot.transpose(1, 0, 2).reshape(rows)
    unit = jnp.arange(units, dtype=jnp.int32)
    unit_first = UNIT * jnp.min(
        jnp.where(unit_ids[:, None] == unit_ids[None, :], unit[None, :], units), axis=1
    )

    def first_of(spots):
        hit = (spots // UNIT)[:, None] == unit[None, :]
        return jnp.sum(jnp.where(hit, unit_first[None, :], 0), axis=1)

    q_first = first_of(q_spot)
    flat = key_spot.reshape(group)
    cq, sq = turns(q_spot - q_first)
    ck, sk = turns(flat - first_of(flat))
    ck, sk = ck.reshape(seqs, rows, HD), sk.reshape(seqs, rows, HD)
    by_chunk = key_spot.reshape(seqs, seqs, chunk).transpose(1, 0, 2).reshape(group)
    kept = (by_chunk[None, :] <= q_spot[:, None]) & (by_chunk[None, :] >= q_first[:, None])
    bias = jnp.where(kept, 0.0, -1e30).astype(jnp.float32)

    whole2 = lambda *shape: pl.BlockSpec(shape, lambda h: (0,) * len(shape))
    out = pl.pallas_call(
        functools.partial(attend, seqs, dps),
        grid=(KVH,),
        in_specs=[
            pl.BlockSpec((rows, per_kv * HD), lambda h: (0, h)),
            pl.BlockSpec((seqs, rows, HD), lambda h: (0, 0, h)),
            pl.BlockSpec((seqs, rows, HD), lambda h: (0, 0, h + KVH)),
            whole2(rows, HD),
            whole2(rows, HD),
            whole2(seqs, rows, HD),
            whole2(seqs, rows, HD),
            whole2(rows, group),
        ],
        out_specs=pl.BlockSpec((rows, per_kv * HD), lambda h: (0, h)),
        out_shape=jax.ShapeDtypeStruct(queries.shape, jnp.bfloat16),
        scratch_shapes=[
            pltpu.VMEM((group, HD), jnp.bfloat16),
            pltpu.VMEM((group, HD), jnp.bfloat16),
            pltpu.VMEM((rows, per_kv * HD), jnp.bfloat16),
        ],
        compiler_params=pltpu.CompilerParams(vmem_limit_bytes=48 * 1024 * 1024),
    )(q_here, kv_all, kv_all, cq, sq, ck, sk, bias)
    home = swap(out)
    return lax.dot_general(
        onehot, home, (((0,), (0,)), ((), ())), preferred_element_type=jnp.float32
    ).astype(jnp.bfloat16)


def solution(mesh):
    return jax.shard_map(
        per_device,
        mesh=mesh,
        in_specs=(
            P(("dp", "seq"), None),
            P(("dp", "seq"), None),
            P(("dp", "seq"), None),
            P(("dp", "seq")),
            P(("dp", "seq")),
        ),
        out_specs=P(("dp", "seq"), None),
        check_vma=False,
    )
```

```python
import functools

import jax
import jax.numpy as jnp
from jax import lax
from jax.experimental import pallas as pl
from jax.experimental.pallas import tpu as pltpu
from jax.sharding import PartitionSpec as P

H = 64
KVH = 8
HD = 128
theta_base = 500000.0
UNIT = 128
META = 128
LOG2E = 1.4426950408889634


def onehot_rows(index, count):
    return (index[None, :] == jnp.arange(count, dtype=jnp.int32)[:, None]).astype(jnp.bfloat16)


def permuted(onehot, rows):
    return jnp.dot(onehot, rows, preferred_element_type=jnp.float32).astype(jnp.bfloat16)


def dot(a, b):
    return jnp.dot(a, b, preferred_element_type=jnp.float32)


def turn(x, c, s):
    return (x * c + pltpu.roll(x, HD // 2, 1) * s).astype(jnp.bfloat16)


def travel(
    seqs, dps, q, kv, seg, freqs, home,
    qr, kvz, metaz, ob, ks, vs, kmeta, cq, sq, ck, sk, bias, part_q,
    kv_send, kv_recv, kv_own, q_send, q_recv, q_own, o_send, o_recv, o_own,
    m_send, m_recv, m_own, mz_send, mz_recv, z_send, z_recv,
):
    rows = q.shape[0]
    per_kv = H // KVH
    wide = per_kv * HD
    chunk = rows // seqs
    share = chunk // dps
    slab = rows // dps
    group = rows * seqs
    upd = rows // UNIT
    me = lax.axis_index("dp")
    z = lax.axis_index("seq")

    def remote(src, dst, send, recv, where):
        return pltpu.make_async_remote_copy(
            src_ref=src, dst_ref=dst, send_sem=send, recv_sem=recv,
            device_id=where, device_id_type=pl.DeviceIdType.MESH,
        )

    barrier = pltpu.get_barrier_semaphore()
    peers = [lax.rem(me + k, dps) for k in range(1, dps)]
    planes = [lax.rem(z + k, seqs) for k in range(1, seqs)]
    for d in peers:
        pl.semaphore_signal(
            barrier, inc=1, device_id=(d, z), device_id_type=pl.DeviceIdType.MESH
        )
    for p in planes:
        pl.semaphore_signal(
            barrier, inc=1, device_id=(me, p), device_id_type=pl.DeviceIdType.MESH
        )
    pl.semaphore_wait(barrier, dps + seqs - 2)

    def slab_of(d):
        return pl.ds(pl.multiple_of(d * slab, slab), slab)

    def cols(h, width):
        return pl.ds(pl.multiple_of(h * width, width), width)

    meta_cols = pl.ds(2 * KVH * HD, META)
    most = pl.ds(0, rows - slab)
    for d in peers:
        remote(
            kv.at[slab_of(d), meta_cols], metaz.at[z, slab_of(me)], m_send, m_recv, (d, z)
        ).start()
    m_copy = pltpu.make_async_copy(
        kv.at[slab_of(me), meta_cols], metaz.at[z, slab_of(me)], m_own.at[0]
    )
    s_copy = pltpu.make_async_copy(seg, metaz.at[z, pl.ds(rows, 16)], m_own.at[1])
    m_copy.start()
    s_copy.start()

    def kv_local(h):
        return pltpu.make_async_copy(
            kv.at[slab_of(me), cols(h, 2 * HD)], kvz.at[z, h, slab_of(me)], kv_own.at[h]
        )

    def q_local(h):
        return pltpu.make_async_copy(
            q.at[slab_of(me), cols(h, wide)], qr.at[h, slab_of(me)], q_own.at[h]
        )

    def o_local(h):
        return pltpu.make_async_copy(
            ob.at[h, slab_of(me)], home.at[slab_of(me), cols(h, wide)], o_own.at[h]
        )

    @pl.loop(0, KVH)
    def _(h):
        for d in peers:
            remote(
                kv.at[slab_of(d), cols(h, 2 * HD)], kvz.at[z, h, slab_of(me)],
                kv_send.at[h], kv_recv.at[h], (d, z),
            ).start()
        kv_local(h).start()

    @pl.loop(0, KVH)
    def _(h):
        for d in peers:
            remote(
                q.at[slab_of(d), cols(h, wide)], qr.at[h, slab_of(me)],
                q_send.at[h], q_recv.at[h], (d, z),
            ).start()
        q_local(h).start()

    def meta_all():
        return remote(metaz.at[z, most], metaz.at[z, most], m_send, m_recv, (me, z))

    def kv_all(h):
        return remote(
            kvz.at[z, h, most], kvz.at[z, h, most], kv_send.at[h], kv_recv.at[h], (me, z)
        )

    def q_all(h):
        return remote(qr.at[h, most], qr.at[h, most], q_send.at[h], q_recv.at[h], (me, z))

    def o_all(h):
        place = home.at[most, cols(h, wide)]
        return remote(ob.at[h, most], place, o_send.at[h], o_recv.at[h], (me, z))

    meta_all().wait_recv()
    m_copy.wait()
    s_copy.wait()

    def meta_hop(k, p, origin):
        return remote(
            metaz.at[origin], metaz.at[origin], mz_send.at[k - 1], mz_recv.at[origin], (me, p)
        )

    for k, p in enumerate(planes, 1):
        meta_hop(k, p, z).start()

    def arrival(s):
        inner = s % chunk
        return (inner // share) * (seqs * share) + (s // chunk) * share + inner % share

    row = lax.broadcasted_iota(jnp.int32, (rows, rows), 0)
    col = lax.broadcasted_iota(jnp.int32, (rows, rows), 1)
    sort = jnp.where(col == arrival(row), 1.0, 0.0).astype(jnp.bfloat16)
    unsort = jnp.where(row == arrival(col), 1.0, 0.0).astype(jnp.bfloat16)

    def prepare():
        for k, p in enumerate(planes, 1):
            meta_hop(k, p, p).wait_recv()
        ids = []
        for p in range(seqs):
            line = metaz[p, rows : rows + 16, :].astype(jnp.float32)
            ids += [line[0:1, u : u + 1] for u in range(upd)]
        lane = lax.broadcasted_iota(jnp.int32, (1, META), 1)
        sign = jnp.where(lane < HD // 2, -1.0, 1.0)

        def spots(sorted_meta):
            spot = sorted_meta[:, 0:1] * 32.0 + sorted_meta[:, 1:2]
            mine = jnp.zeros_like(spot)
            for u in range(len(ids)):
                inside = (spot >= u * UNIT) & (spot < (u + 1) * UNIT)
                mine = jnp.where(inside, ids[u], mine)
            first = jnp.full_like(spot, float(group))
            for u in range(len(ids)):
                first = jnp.where(mine == ids[u], jnp.minimum(first, float(u * UNIT)), first)
            angles = (spot - first) * freqs[0:1, :]
            return spot, first, jnp.cos(angles), jnp.sin(angles) * sign

        for p in range(seqs):
            sorted_meta = dot(sort, metaz[p, :rows, :])
            _, _, ck[p], sk[p] = spots(sorted_meta)
            narrow = sorted_meta.astype(jnp.bfloat16)
            for c in range(seqs):
                kmeta[c * rows + p * chunk : c * rows + (p + 1) * chunk] = narrow[
                    c * chunk : (c + 1) * chunk
                ]
        spot, first, cq[...], sq[...] = spots(dot(sort, metaz[z, :rows, :]))
        weigh = jnp.where(lane == 0, 32.0, jnp.where(lane == 1, 1.0, 0.0))
        weigh = jnp.broadcast_to(weigh, (16, META)).astype(jnp.bfloat16)
        key = lax.dot_general(
            weigh, kmeta[...], (((1,), (1,)), ((), ())), preferred_element_type=jnp.float32
        )[0:1, :]
        bias[...] = jnp.where((key <= spot) & (key >= first), 0.0, -1e30)

    def attend(h):
        for p in range(seqs):
            both = dot(sort, kvz[p, h])
            part = turn(both[:, :HD], ck[p], sk[p])
            part_v = both[:, HD:].astype(jnp.bfloat16)
            for c in range(seqs):
                place = slice(c * rows + p * chunk, c * rows + (p + 1) * chunk)
                ks[place] = part[c * chunk : (c + 1) * chunk]
                vs[place] = part_v[c * chunk : (c + 1) * chunk]
        x = dot(sort, qr[h])
        turned = [turn(x[:, g * HD : (g + 1) * HD], cq[...], sq[...]) for g in range(per_kv)]
        for c in range(seqs):
            reach = (c + 1) * rows
            block = jnp.concatenate([t[c * chunk : (c + 1) * chunk] for t in turned], axis=0)
            s = lax.dot_general(
                block, ks[:reach], (((1,), (1,)), ((), ())), preferred_element_type=jnp.float32
            )
            s = s.reshape(per_kv, chunk, reach) * (HD ** -0.5 * LOG2E)
            s = s + bias[c * chunk : (c + 1) * chunk, :reach][None]
            e = jnp.exp2(s - jnp.max(s, axis=-1, keepdims=True))
            total = jnp.sum(e, axis=-1, keepdims=True).reshape(per_kv * chunk, 1)
            mixed = dot(e.astype(jnp.bfloat16).reshape(per_kv * chunk, reach), vs[:reach])
            mixed = (mixed / total).astype(jnp.bfloat16)
            for g in range(per_kv):
                part_q[c * chunk : (c + 1) * chunk, g * HD : (g + 1) * HD] = mixed[
                    g * chunk : (g + 1) * chunk
                ]
        ob[h] = dot(unsort, part_q[...]).astype(jnp.bfloat16)

    def hop(up, t, origin, h):
        step = 1 if up else -1
        return remote(
            kvz.at[origin, h], kvz.at[origin, h],
            z_send.at[(0 if up else 1) * seqs + t, h], z_recv.at[origin, h], (me, z + step),
        )

    @pl.loop(0, KVH + seqs - 1)
    def _(i):
        @pl.when(i < KVH)
        def _():
            kv_all(i).wait_recv()
            kv_local(i).wait()

            @pl.when(z + 1 < seqs)
            def _():
                hop(True, 0, z, i).start()

            @pl.when(z > 0)
            def _():
                hop(False, 0, z, i).start()

        for t in range(1, seqs):
            live = (i >= t) & (i - t < KVH)

            @pl.when(live & (z >= t))
            def _():
                hop(True, t, z - t, i - t).wait_recv()

                @pl.when(z + 1 < seqs)
                def _():
                    hop(True, t, z - t, i - t).start()

            @pl.when(live & (z + t < seqs))
            def _():
                hop(False, t, z + t, i - t).wait_recv()

                @pl.when(z > 0)
                def _():
                    hop(False, t, z + t, i - t).start()

        @pl.when(i == 1)
        def _():
            prepare()

        @pl.when(i >= seqs - 1)
        def _():
            h = i - (seqs - 1)
            q_all(h).wait_recv()
            q_local(h).wait()
            attend(h)
            for d in peers:
                remote(
                    ob.at[h, slab_of(d)], home.at[slab_of(me), cols(h, wide)],
                    o_send.at[h], o_recv.at[h], (d, z),
                ).start()
            o_local(h).start()

    meta_all().wait_send()
    for k, p in enumerate(planes, 1):
        meta_hop(k, p, z).wait_send()

    @pl.loop(0, KVH)
    def _(h):
        kv_all(h).wait_send()
        q_all(h).wait_send()
        for t in range(seqs - 1):

            @pl.when((z >= t) & (z + 1 < seqs))
            def _():
                hop(True, t, z - t, h).wait_send()

            @pl.when((z + t < seqs) & (z > 0))
            def _():
                hop(False, t, z + t, h).wait_send()

        o_all(h).wait_send()
        o_all(h).wait_recv()
        o_local(h).wait()


def per_device(queries, keys, values, plan, segment_ids):
    rows = queries.shape[0]
    seqs = lax.axis_size("seq")
    dps = lax.axis_size("dp")
    group = rows * seqs
    share = rows // (seqs * dps)
    chunk = rows // seqs
    per_kv = H // KVH
    target = plan // rows
    places = jnp.arange(rows, dtype=jnp.int32)
    same = (target[:, None] == target[None, :]) & (places[None, :] < places[:, None])
    slot = target * share + jnp.sum(same.astype(jnp.int32), axis=1)
    onehot = onehot_rows(slot, rows)
    spot = plan % group
    lane = jnp.arange(META, dtype=jnp.int32)[None, :]
    meta = jnp.where(lane == 0, (spot // 32)[:, None], jnp.where(lane == 1, (spot % 32)[:, None], 0))
    pairs = jnp.concatenate([keys.reshape(rows, KVH, HD), values.reshape(rows, KVH, HD)], axis=2)
    kv = jnp.concatenate([pairs.reshape(rows, 2 * KVH * HD), meta.astype(jnp.bfloat16)], axis=1)
    units = segment_ids[::UNIT]
    seg = jnp.zeros((16, META), jnp.bfloat16).at[0, : units.shape[0]].set(units.astype(jnp.bfloat16))
    exponents = jnp.arange(HD // 2, dtype=jnp.float32)
    freqs = theta_base ** (-2.0 * exponents / HD)
    freqs = jnp.broadcast_to(jnp.concatenate([freqs, freqs])[None, :], (8, HD))
    anywhere = pl.BlockSpec(memory_space=pl.ANY)
    inside = pl.BlockSpec(memory_space=pltpu.VMEM)
    dma = pltpu.SemaphoreType.DMA
    bf16, f32 = jnp.bfloat16, jnp.float32
    home = pl.pallas_call(
        functools.partial(travel, seqs, dps),
        in_specs=[anywhere, anywhere, inside, inside],
        out_specs=anywhere,
        out_shape=jax.ShapeDtypeStruct(queries.shape, bf16),
        scratch_shapes=[
            pltpu.VMEM((KVH, rows, per_kv * HD), bf16),
            pltpu.VMEM((seqs, KVH, rows, 2 * HD), bf16),
            pltpu.VMEM((seqs, rows + 16, META), bf16),
            pltpu.VMEM((KVH, rows, per_kv * HD), bf16),
            pltpu.VMEM((group, HD), bf16),
            pltpu.VMEM((group, HD), bf16),
            pltpu.VMEM((group, META), bf16),
            pltpu.VMEM((rows, HD), f32),
            pltpu.VMEM((rows, HD), f32),
            pltpu.VMEM((seqs, rows, HD), f32),
            pltpu.VMEM((seqs, rows, HD), f32),
            pltpu.VMEM((rows, group), f32),
            pltpu.VMEM((rows, per_kv * HD), bf16),
            dma((KVH,)), dma((KVH,)), dma((KVH,)),
            dma((KVH,)), dma((KVH,)), dma((KVH,)),
            dma((KVH,)), dma((KVH,)), dma((KVH,)),
            dma, dma, dma((2,)), dma((seqs,)), dma((seqs,)),
            dma((2 * seqs, KVH)), dma((seqs, KVH)),
        ],
        compiler_params=pltpu.CompilerParams(
            collective_id=0, has_side_effects=True, vmem_limit_bytes=56 * 1024 * 1024
        ),
    )(permuted(onehot, queries), permuted(onehot, kv), seg, freqs)
    return lax.dot_general(
        onehot, home, (((0,), (0,)), ((), ())), preferred_element_type=jnp.float32
    ).astype(jnp.bfloat16)


def solution(mesh):
    return jax.shard_map(
        per_device,
        mesh=mesh,
        in_specs=(
            P(("dp", "seq"), None),
            P(("dp", "seq"), None),
            P(("dp", "seq"), None),
            P(("dp", "seq")),
            P(("dp", "seq")),
        ),
        out_specs=P(("dp", "seq"), None),
        check_vma=False,
    )
```

```python
import functools

import jax
import jax.numpy as jnp
import numpy as np
from jax import lax
from jax.experimental import pallas as pl
from jax.experimental.pallas import tpu as pltpu
from jax.sharding import PartitionSpec as P

H = 64
KVH = 8
HD = 128
theta_base = 500000.0
UNIT = 128
META = 128
LOG2E = 1.4426950408889634


def dot(a, b):
    return jnp.dot(a, b, preferred_element_type=jnp.float32)


def turn(x, c, s):
    return (x * c + pltpu.roll(x, HD // 2, 1) * s).astype(jnp.bfloat16)


def restore(onehot, home, out):
    out[...] = lax.dot_general(
        onehot[...], home[...], (((0,), (0,)), ((), ())), preferred_element_type=jnp.float32
    ).astype(jnp.bfloat16)


def travel(
    seqs, dps, q, k, v, plan, seg, freqs, home, onehot,
    qs, kvs, metas, qr, kvz, metaz, ob, ks, vs, kmeta, cq, sq, ck, sk, bias, part_q,
    kv_send, kv_recv, kv_own, q_send, q_recv, q_own, q_load, o_send, o_recv, o_own,
    m_send, m_recv, m_own, mz_send, mz_recv, z_send, z_recv,
):
    rows = q.shape[0]
    per_kv = H // KVH
    wide = per_kv * HD
    chunk = rows // seqs
    share = chunk // dps
    slab = rows // dps
    group = rows * seqs
    upd = rows // UNIT
    me = lax.axis_index("dp")
    z = lax.axis_index("seq")

    def remote(src, dst, send, recv, where):
        return pltpu.make_async_remote_copy(
            src_ref=src, dst_ref=dst, send_sem=send, recv_sem=recv,
            device_id=where, device_id_type=pl.DeviceIdType.MESH,
        )

    def slab_of(d):
        return pl.ds(pl.multiple_of(d * slab, slab), slab)

    def cols(h, width):
        return pl.ds(pl.multiple_of(h * width, width), width)

    barrier = pltpu.get_barrier_semaphore()
    peers = [lax.rem(me + k, dps) for k in range(1, dps)]
    planes = [lax.rem(z + k, seqs) for k in range(1, seqs)]
    for d in peers:
        pl.semaphore_signal(
            barrier, inc=1, device_id=(d, z), device_id_type=pl.DeviceIdType.MESH
        )
    for p in planes:
        pl.semaphore_signal(
            barrier, inc=1, device_id=(me, p), device_id_type=pl.DeviceIdType.MESH
        )

    def q_in(h):
        return pltpu.make_async_copy(q.at[:, cols(h, wide)], qs.at[h], q_load.at[h])

    @pl.loop(0, KVH)
    def _(h):
        q_in(h).start()

    row = lax.broadcasted_iota(jnp.int32, (rows, rows), 0)
    col = lax.broadcasted_iota(jnp.int32, (rows, rows), 1)
    eye = jnp.where(row == col, 1.0, 0.0).astype(jnp.bfloat16)
    target = (plan[...] // rows).astype(jnp.float32)
    spread = jnp.broadcast_to(target, (16, rows)).astype(jnp.bfloat16)
    across = (((1,), (1,)), ((), ()))
    upright = lax.dot_general(eye, spread, across, preferred_element_type=jnp.float32)[:, 0:1]
    ahead = jnp.where((upright == target) & (row < col), 1.0, 0.0)
    slot = target * share + jnp.sum(ahead, axis=0, keepdims=True)
    onehot[...] = jnp.where(slot == row.astype(jnp.float32), 1.0, 0.0).astype(jnp.bfloat16)
    spot_row = plan[...] % group
    lines = lax.broadcasted_iota(jnp.int32, (META, rows), 0)
    high = (spot_row // 32).astype(jnp.float32)
    low = (spot_row % 32).astype(jnp.float32)
    lines = jnp.where(lines == 0, high, jnp.where(lines == 1, low, 0.0)).astype(jnp.bfloat16)
    metas[...] = lax.dot_general(
        onehot[...], lines, across, preferred_element_type=jnp.float32
    ).astype(jnp.bfloat16)
    lane = lax.broadcasted_iota(jnp.int32, (1, META), 1)
    marks = jnp.zeros((1, META), jnp.float32)
    for u in range(upd):
        marks = jnp.where(lane == u, seg[0:1, u * UNIT : u * UNIT + 1].astype(jnp.float32), marks)
    metaz[z, rows : rows + 16, :] = jnp.broadcast_to(marks, (16, META)).astype(jnp.bfloat16)

    pl.semaphore_wait(barrier, dps + seqs - 2)

    most = pl.ds(0, rows - slab)
    for d in peers:
        remote(
            metas.at[slab_of(d)], metaz.at[z, slab_of(me)], m_send, m_recv, (d, z)
        ).start()
    m_copy = pltpu.make_async_copy(metas.at[slab_of(me)], metaz.at[z, slab_of(me)], m_own)
    m_copy.start()

    def kv_local(h):
        return pltpu.make_async_copy(
            kvs.at[h, slab_of(me)], kvz.at[z, h, slab_of(me)], kv_own.at[h]
        )

    def q_local(h):
        return pltpu.make_async_copy(
            qs.at[h, slab_of(me)], qr.at[h, slab_of(me)], q_own.at[h]
        )

    def o_local(h):
        return pltpu.make_async_copy(
            ob.at[h, slab_of(me)], home.at[slab_of(me), cols(h, wide)], o_own.at[h]
        )

    @pl.loop(0, KVH)
    def _(h):
        both = jnp.concatenate([k[:, cols(h, HD)], v[:, cols(h, HD)]], axis=1)
        kvs[h] = dot(onehot[...], both).astype(jnp.bfloat16)
        for d in peers:
            remote(
                kvs.at[h, slab_of(d)], kvz.at[z, h, slab_of(me)],
                kv_send.at[h], kv_recv.at[h], (d, z),
            ).start()
        kv_local(h).start()

    def q_out(h):
        q_in(h).wait()
        qs[h] = dot(onehot[...], qs[h]).astype(jnp.bfloat16)
        for d in peers:
            remote(
                qs.at[h, slab_of(d)], qr.at[h, slab_of(me)],
                q_send.at[h], q_recv.at[h], (d, z),
            ).start()
        q_local(h).start()

    def meta_all():
        return remote(metaz.at[z, most], metaz.at[z, most], m_send, m_recv, (me, z))

    def kv_all(h):
        return remote(
            kvz.at[z, h, most], kvz.at[z, h, most], kv_send.at[h], kv_recv.at[h], (me, z)
        )

    def q_all(h):
        return remote(qr.at[h, most], qr.at[h, most], q_send.at[h], q_recv.at[h], (me, z))

    def o_all(h):
        place = home.at[most, cols(h, wide)]
        return remote(ob.at[h, most], place, o_send.at[h], o_recv.at[h], (me, z))

    meta_all().wait_recv()
    m_copy.wait()

    def meta_hop(k, p, origin):
        return remote(
            metaz.at[origin], metaz.at[origin], mz_send.at[k - 1], mz_recv.at[origin], (me, p)
        )

    for k, p in enumerate(planes, 1):
        meta_hop(k, p, z).start()

    def arrival(s):
        inner = s % chunk
        return (inner // share) * (seqs * share) + (s // chunk) * share + inner % share

    sort = jnp.where(col == arrival(row), 1.0, 0.0).astype(jnp.bfloat16)
    unsort = jnp.where(row == arrival(col), 1.0, 0.0).astype(jnp.bfloat16)

    def prepare():
        for k, p in enumerate(planes, 1):
            meta_hop(k, p, p).wait_recv()
        ids = []
        for p in range(seqs):
            line = metaz[p, rows : rows + 16, :].astype(jnp.float32)
            ids += [line[0:1, u : u + 1] for u in range(upd)]
        sign = jnp.where(lane < HD // 2, -1.0, 1.0)

        def spots(sorted_meta):
            spot = sorted_meta[:, 0:1] * 32.0 + sorted_meta[:, 1:2]
            mine = jnp.zeros_like(spot)
            for u in range(len(ids)):
                inside = (spot >= u * UNIT) & (spot < (u + 1) * UNIT)
                mine = jnp.where(inside, ids[u], mine)
            first = jnp.full_like(spot, float(group))
            for u in range(len(ids)):
                first = jnp.where(mine == ids[u], jnp.minimum(first, float(u * UNIT)), first)
            angles = (spot - first) * freqs[0:1, :]
            return spot, first, jnp.cos(angles), jnp.sin(angles) * sign

        for p in range(seqs):
            sorted_meta = dot(sort, metaz[p, :rows, :])
            _, _, ck[p], sk[p] = spots(sorted_meta)
            narrow = sorted_meta.astype(jnp.bfloat16)
            for c in range(seqs):
                kmeta[c * rows + p * chunk : c * rows + (p + 1) * chunk] = narrow[
                    c * chunk : (c + 1) * chunk
                ]
        spot, first, cq[...], sq[...] = spots(dot(sort, metaz[z, :rows, :]))
        weigh = jnp.where(lane == 0, 32.0, jnp.where(lane == 1, 1.0, 0.0))
        weigh = jnp.broadcast_to(weigh, (16, META)).astype(jnp.bfloat16)
        key = lax.dot_general(
            weigh, kmeta[...], (((1,), (1,)), ((), ())), preferred_element_type=jnp.float32
        )[0:1, :]
        bias[...] = jnp.where((key <= spot) & (key >= first), 0.0, -1e30)

    def attend(h):
        for p in range(seqs):
            both = dot(sort, kvz[p, h])
            part = turn(both[:, :HD], ck[p], sk[p])
            part_v = both[:, HD:].astype(jnp.bfloat16)
            for c in range(seqs):
                place = slice(c * rows + p * chunk, c * rows + (p + 1) * chunk)
                ks[place] = part[c * chunk : (c + 1) * chunk]
                vs[place] = part_v[c * chunk : (c + 1) * chunk]
        x = dot(sort, qr[h])
        turned = [turn(x[:, g * HD : (g + 1) * HD], cq[...], sq[...]) for g in range(per_kv)]
        for c in range(seqs):
            reach = (c + 1) * rows
            block = jnp.concatenate([t[c * chunk : (c + 1) * chunk] for t in turned], axis=0)
            s = lax.dot_general(
                block, ks[:reach], (((1,), (1,)), ((), ())), preferred_element_type=jnp.float32
            )
            s = s.reshape(per_kv, chunk, reach) * (HD ** -0.5 * LOG2E)
            s = s + bias[c * chunk : (c + 1) * chunk, :reach][None]
            e = jnp.exp2(s - jnp.max(s, axis=-1, keepdims=True))
            total = jnp.sum(e, axis=-1, keepdims=True).reshape(per_kv * chunk, 1)
            mixed = dot(e.astype(jnp.bfloat16).reshape(per_kv * chunk, reach), vs[:reach])
            mixed = (mixed / total).astype(jnp.bfloat16)
            for g in range(per_kv):
                part_q[c * chunk : (c + 1) * chunk, g * HD : (g + 1) * HD] = mixed[
                    g * chunk : (g + 1) * chunk
                ]
        ob[h] = dot(unsort, part_q[...]).astype(jnp.bfloat16)

    def hop(up, t, origin, h):
        step = 1 if up else -1
        return remote(
            kvz.at[origin, h], kvz.at[origin, h],
            z_send.at[(0 if up else 1) * seqs + t, h], z_recv.at[origin, h], (me, z + step),
        )

    @pl.loop(0, KVH + seqs - 1)
    def _(i):
        @pl.when(i < KVH)
        def _():
            kv_all(i).wait_recv()
            kv_local(i).wait()

            @pl.when(z + 1 < seqs)
            def _():
                hop(True, 0, z, i).start()

            @pl.when(z > 0)
            def _():
                hop(False, 0, z, i).start()

        for t in range(1, seqs):
            live = (i >= t) & (i - t < KVH)

            @pl.when(live & (z >= t))
            def _():
                hop(True, t, z - t, i - t).wait_recv()

                @pl.when(z + 1 < seqs)
                def _():
                    hop(True, t, z - t, i - t).start()

            @pl.when(live & (z + t < seqs))
            def _():
                hop(False, t, z + t, i - t).wait_recv()

                @pl.when(z > 0)
                def _():
                    hop(False, t, z + t, i - t).start()

        @pl.when(i < KVH // 2)
        def _():
            q_out(2 * i)
            q_out(2 * i + 1)

        @pl.when(i == min(2, seqs - 1))
        def _():
            prepare()

        @pl.when(i >= seqs - 1)
        def _():
            h = i - (seqs - 1)
            q_all(h).wait_recv()
            q_local(h).wait()
            attend(h)
            for d in peers:
                remote(
                    ob.at[h, slab_of(d)], home.at[slab_of(me), cols(h, wide)],
                    o_send.at[h], o_recv.at[h], (d, z),
                ).start()
            o_local(h).start()

    meta_all().wait_send()
    for k, p in enumerate(planes, 1):
        meta_hop(k, p, z).wait_send()

    @pl.loop(0, KVH)
    def _(h):
        kv_all(h).wait_send()
        q_all(h).wait_send()
        for t in range(seqs - 1):

            @pl.when((z >= t) & (z + 1 < seqs))
            def _():
                hop(True, t, z - t, h).wait_send()

            @pl.when((z + t < seqs) & (z > 0))
            def _():
                hop(False, t, z + t, h).wait_send()

        o_all(h).wait_send()
        o_all(h).wait_recv()
        o_local(h).wait()


def per_device(queries, keys, values, plan, segment_ids):
    rows = queries.shape[0]
    seqs = lax.axis_size("seq")
    dps = lax.axis_size("dp")
    group = rows * seqs
    share = rows // (seqs * dps)
    chunk = rows // seqs
    per_kv = H // KVH
    exponents = np.arange(HD // 2, dtype=np.float32)
    freqs = np.float32(theta_base) ** (np.float32(-2.0) * exponents / np.float32(HD))
    freqs = jnp.asarray(np.broadcast_to(np.concatenate([freqs, freqs])[None, :], (8, HD)))
    anywhere = pl.BlockSpec(memory_space=pl.ANY)
    inside = pl.BlockSpec(memory_space=pltpu.VMEM)
    dma = pltpu.SemaphoreType.DMA
    bf16, f32 = jnp.bfloat16, jnp.float32
    home, onehot = pl.pallas_call(
        functools.partial(travel, seqs, dps),
        in_specs=[anywhere, inside, inside, inside, inside, inside],
        out_specs=(anywhere, inside),
        out_shape=(
            jax.ShapeDtypeStruct(queries.shape, bf16),
            jax.ShapeDtypeStruct((rows, rows), bf16),
        ),
        scratch_shapes=[
            pltpu.VMEM((KVH, rows, per_kv * HD), bf16),
            pltpu.VMEM((KVH, rows, 2 * HD), bf16),
            pltpu.VMEM((rows, META), bf16),
            pltpu.VMEM((KVH, rows, per_kv * HD), bf16),
            pltpu.VMEM((seqs, KVH, rows, 2 * HD), bf16),
            pltpu.VMEM((seqs, rows + 16, META), bf16),
            pltpu.VMEM((KVH, rows, per_kv * HD), bf16),
            pltpu.VMEM((group, HD), bf16),
            pltpu.VMEM((group, HD), bf16),
            pltpu.VMEM((group, META), bf16),
            pltpu.VMEM((rows, HD), f32),
            pltpu.VMEM((rows, HD), f32),
            pltpu.VMEM((seqs, rows, HD), f32),
            pltpu.VMEM((seqs, rows, HD), f32),
            pltpu.VMEM((rows, group), f32),
            pltpu.VMEM((rows, per_kv * HD), bf16),
            dma((KVH,)), dma((KVH,)), dma((KVH,)),
            dma((KVH,)), dma((KVH,)), dma((KVH,)),
            dma((KVH,)), dma((KVH,)), dma((KVH,)), dma((KVH,)),
            dma, dma, dma, dma((seqs,)), dma((seqs,)),
            dma((2 * seqs, KVH)), dma((seqs, KVH)),
        ],
        compiler_params=pltpu.CompilerParams(
            collective_id=0, has_side_effects=True, vmem_limit_bytes=56 * 1024 * 1024
        ),
    )(queries, keys, values, plan[None, :], segment_ids[None, :], freqs)
    block = pl.BlockSpec((rows, per_kv * HD), lambda h: (0, h))
    return pl.pallas_call(
        restore,
        grid=(KVH,),
        in_specs=[pl.BlockSpec((rows, rows), lambda h: (0, 0)), block],
        out_specs=block,
        out_shape=jax.ShapeDtypeStruct(queries.shape, bf16),
    )(onehot, home)


def solution(mesh):
    return jax.shard_map(
        per_device,
        mesh=mesh,
        in_specs=(
            P(("dp", "seq"), None),
            P(("dp", "seq"), None),
            P(("dp", "seq"), None),
            P(("dp", "seq")),
            P(("dp", "seq")),
        ),
        out_specs=P(("dp", "seq"), None),
        check_vma=False,
    )
```

```python
import functools

import jax
import jax.numpy as jnp
import numpy as np
from jax import lax
from jax.experimental import pallas as pl
from jax.experimental.pallas import tpu as pltpu
from jax.sharding import PartitionSpec as P

H = 64
KVH = 8
HD = 128
theta_base = 500000.0
UNIT = 128
AHEAD = 2
META = 128
LOG2E = 1.4426950408889634


def dot(a, b):
    return jnp.dot(a, b, preferred_element_type=jnp.float32)


def turn(x, c, s):
    return (x * c + pltpu.roll(x, HD // 2, 1) * s).astype(jnp.bfloat16)


def restore(onehot, home, out):
    out[...] = lax.dot_general(
        onehot[...], home[...], (((0,), (0,)), ((), ())), preferred_element_type=jnp.float32
    ).astype(jnp.bfloat16)


def travel(
    seqs, dps, q, k, v, plan, seg, freqs, home, onehot,
    qs, kvs, metas, qr, kvz, metaz, ob, ks, vs, kmeta, cq, sq, ck, sk, bias, part_q,
    kv_send, kv_recv, kv_own, q_send, q_recv, q_own, q_load, o_send, o_recv, o_own,
    m_send, m_recv, m_own, mz_send, mz_recv, z_send, z_recv,
):
    rows = q.shape[0]
    per_kv = H // KVH
    wide = per_kv * HD
    chunk = rows // seqs
    share = chunk // dps
    slab = rows // dps
    group = rows * seqs
    upd = rows // UNIT
    me = lax.axis_index("dp")
    z = lax.axis_index("seq")

    def remote(src, dst, send, recv, where):
        return pltpu.make_async_remote_copy(
            src_ref=src, dst_ref=dst, send_sem=send, recv_sem=recv,
            device_id=where, device_id_type=pl.DeviceIdType.MESH,
        )

    def slab_of(d):
        return pl.ds(pl.multiple_of(d * slab, slab), slab)

    def cols(h, width):
        return pl.ds(pl.multiple_of(h * width, width), width)

    barrier = pltpu.get_barrier_semaphore()
    peers = [lax.rem(me + k, dps) for k in range(1, dps)]
    planes = [lax.rem(z + k, seqs) for k in range(1, seqs)]
    for d in peers:
        pl.semaphore_signal(
            barrier, inc=1, device_id=(d, z), device_id_type=pl.DeviceIdType.MESH
        )
    for p in planes:
        pl.semaphore_signal(
            barrier, inc=1, device_id=(me, p), device_id_type=pl.DeviceIdType.MESH
        )

    def q_in(h):
        return pltpu.make_async_copy(q.at[:, cols(h, wide)], qs.at[h], q_load.at[h])

    @pl.loop(0, KVH)
    def _(h):
        q_in(h).start()

    row = lax.broadcasted_iota(jnp.int32, (rows, rows), 0)
    col = lax.broadcasted_iota(jnp.int32, (rows, rows), 1)
    eye = jnp.where(row == col, 1.0, 0.0).astype(jnp.bfloat16)
    target = (plan[...] // rows).astype(jnp.float32)
    spread = jnp.broadcast_to(target, (16, rows)).astype(jnp.bfloat16)
    across = (((1,), (1,)), ((), ()))
    upright = lax.dot_general(eye, spread, across, preferred_element_type=jnp.float32)[:, 0:1]
    ahead = jnp.where((upright == target) & (row < col), 1.0, 0.0)
    slot = target * share + jnp.sum(ahead, axis=0, keepdims=True)
    onehot[...] = jnp.where(slot == row.astype(jnp.float32), 1.0, 0.0).astype(jnp.bfloat16)
    spot_row = plan[...] % group
    lines = lax.broadcasted_iota(jnp.int32, (META, rows), 0)
    high = (spot_row // 32).astype(jnp.float32)
    low = (spot_row % 32).astype(jnp.float32)
    lines = jnp.where(lines == 0, high, jnp.where(lines == 1, low, 0.0)).astype(jnp.bfloat16)
    metas[...] = lax.dot_general(
        onehot[...], lines, across, preferred_element_type=jnp.float32
    ).astype(jnp.bfloat16)
    lane = lax.broadcasted_iota(jnp.int32, (1, META), 1)
    marks = jnp.zeros((1, META), jnp.float32)
    for u in range(upd):
        marks = jnp.where(lane == u, seg[0:1, u * UNIT : u * UNIT + 1].astype(jnp.float32), marks)
    metaz[z, rows : rows + 16, :] = jnp.broadcast_to(marks, (16, META)).astype(jnp.bfloat16)

    pl.semaphore_wait(barrier, dps + seqs - 2)

    most = pl.ds(0, rows - slab)
    for d in peers:
        remote(
            metas.at[slab_of(d)], metaz.at[z, slab_of(me)], m_send, m_recv, (d, z)
        ).start()
    m_copy = pltpu.make_async_copy(metas.at[slab_of(me)], metaz.at[z, slab_of(me)], m_own)
    m_copy.start()

    def kv_local(h):
        return pltpu.make_async_copy(
            kvs.at[h, slab_of(me)], kvz.at[z, h, slab_of(me)], kv_own.at[h]
        )

    def q_local(h):
        return pltpu.make_async_copy(
            qs.at[h, slab_of(me)], qr.at[h, slab_of(me)], q_own.at[h]
        )

    def o_local(h):
        return pltpu.make_async_copy(
            ob.at[h, slab_of(me)], home.at[slab_of(me), cols(h, wide)], o_own.at[h]
        )

    @pl.loop(0, KVH)
    def _(h):
        both = jnp.concatenate([k[:, cols(h, HD)], v[:, cols(h, HD)]], axis=1)
        kvs[h] = dot(onehot[...], both).astype(jnp.bfloat16)
        for d in peers:
            remote(
                kvs.at[h, slab_of(d)], kvz.at[z, h, slab_of(me)],
                kv_send.at[h], kv_recv.at[h], (d, z),
            ).start()
        kv_local(h).start()

    def q_out(h):
        q_in(h).wait()
        qs[h] = dot(onehot[...], qs[h]).astype(jnp.bfloat16)
        for d in peers:
            remote(
                qs.at[h, slab_of(d)], qr.at[h, slab_of(me)],
                q_send.at[h], q_recv.at[h], (d, z),
            ).start()
        q_local(h).start()

    def meta_all():
        return remote(metaz.at[z, most], metaz.at[z, most], m_send, m_recv, (me, z))

    def kv_all(h):
        return remote(
            kvz.at[z, h, most], kvz.at[z, h, most], kv_send.at[h], kv_recv.at[h], (me, z)
        )

    def q_all(h):
        return remote(qr.at[h, most], qr.at[h, most], q_send.at[h], q_recv.at[h], (me, z))

    def o_all(h):
        place = home.at[most, cols(h, wide)]
        return remote(ob.at[h, most], place, o_send.at[h], o_recv.at[h], (me, z))

    meta_all().wait_recv()
    m_copy.wait()

    def meta_hop(k, p, origin):
        return remote(
            metaz.at[origin], metaz.at[origin], mz_send.at[k - 1], mz_recv.at[origin], (me, p)
        )

    for k, p in enumerate(planes, 1):
        meta_hop(k, p, z).start()

    def arrival(s):
        inner = s % chunk
        return (inner // share) * (seqs * share) + (s // chunk) * share + inner % share

    sort = jnp.where(col == arrival(row), 1.0, 0.0).astype(jnp.bfloat16)
    unsort = jnp.where(row == arrival(col), 1.0, 0.0).astype(jnp.bfloat16)

    def prepare():
        for k, p in enumerate(planes, 1):
            meta_hop(k, p, p).wait_recv()
        ids = []
        for p in range(seqs):
            line = metaz[p, rows : rows + 16, :].astype(jnp.float32)
            ids += [line[0:1, u : u + 1] for u in range(upd)]
        sign = jnp.where(lane < HD // 2, -1.0, 1.0)

        def spots(sorted_meta):
            spot = sorted_meta[:, 0:1] * 32.0 + sorted_meta[:, 1:2]
            mine = jnp.zeros_like(spot)
            for u in range(len(ids)):
                inside = (spot >= u * UNIT) & (spot < (u + 1) * UNIT)
                mine = jnp.where(inside, ids[u], mine)
            first = jnp.full_like(spot, float(group))
            for u in range(len(ids)):
                first = jnp.where(mine == ids[u], jnp.minimum(first, float(u * UNIT)), first)
            angles = (spot - first) * freqs[0:1, :]
            return spot, first, jnp.cos(angles), jnp.sin(angles) * sign

        for p in range(seqs):
            sorted_meta = dot(sort, metaz[p, :rows, :])
            _, _, ck[p], sk[p] = spots(sorted_meta)
            narrow = sorted_meta.astype(jnp.bfloat16)
            for c in range(seqs):
                kmeta[c * rows + p * chunk : c * rows + (p + 1) * chunk] = narrow[
                    c * chunk : (c + 1) * chunk
                ]
        spot, first, cq[...], sq[...] = spots(dot(sort, metaz[z, :rows, :]))
        weigh = jnp.where(lane == 0, 32.0, jnp.where(lane == 1, 1.0, 0.0))
        weigh = jnp.broadcast_to(weigh, (16, META)).astype(jnp.bfloat16)
        key = lax.dot_general(
            weigh, kmeta[...], (((1,), (1,)), ((), ())), preferred_element_type=jnp.float32
        )[0:1, :]
        bias[...] = jnp.where((key <= spot) & (key >= first), 0.0, -1e30)

    def attend(h):
        for p in range(seqs):
            both = dot(sort, kvz[p, h])
            part = turn(both[:, :HD], ck[p], sk[p])
            part_v = both[:, HD:].astype(jnp.bfloat16)
            for c in range(seqs):
                place = slice(c * rows + p * chunk, c * rows + (p + 1) * chunk)
                ks[place] = part[c * chunk : (c + 1) * chunk]
                vs[place] = part_v[c * chunk : (c + 1) * chunk]
        x = dot(sort, qr[h])
        turned = [turn(x[:, g * HD : (g + 1) * HD], cq[...], sq[...]) for g in range(per_kv)]
        for c in range(seqs):
            reach = (c + 1) * rows
            block = jnp.concatenate([t[c * chunk : (c + 1) * chunk] for t in turned], axis=0)
            s = lax.dot_general(
                block, ks[:reach], (((1,), (1,)), ((), ())), preferred_element_type=jnp.float32
            )
            s = s.reshape(per_kv, chunk, reach) * (HD ** -0.5 * LOG2E)
            s = s + bias[c * chunk : (c + 1) * chunk, :reach][None]
            e = jnp.exp2(s - jnp.max(s, axis=-1, keepdims=True))
            total = jnp.sum(e, axis=-1, keepdims=True).reshape(per_kv * chunk, 1)
            mixed = dot(e.astype(jnp.bfloat16).reshape(per_kv * chunk, reach), vs[:reach])
            mixed = (mixed / total).astype(jnp.bfloat16)
            for g in range(per_kv):
                part_q[c * chunk : (c + 1) * chunk, g * HD : (g + 1) * HD] = mixed[
                    g * chunk : (g + 1) * chunk
                ]
        ob[h] = dot(unsort, part_q[...]).astype(jnp.bfloat16)

    def hop(up, t, origin, h):
        step = 1 if up else -1
        return remote(
            kvz.at[origin, h], kvz.at[origin, h],
            z_send.at[(0 if up else 1) * seqs + t, h], z_recv.at[origin, h], (me, z + step),
        )

    @pl.loop(0, KVH + seqs - 1)
    def _(i):
        @pl.when(i < KVH // AHEAD)
        def _():
            for n in range(AHEAD):
                h = i * AHEAD + n
                kv_all(h).wait_recv()
                kv_local(h).wait()

                @pl.when(z + 1 < seqs)
                def _():
                    hop(True, 0, z, h).start()

                @pl.when(z > 0)
                def _():
                    hop(False, 0, z, h).start()

        for t in range(1, seqs):
            live = (i >= t) & (i - t < KVH)

            @pl.when(live & (z >= t))
            def _():
                hop(True, t, z - t, i - t).wait_recv()

                @pl.when(z + 1 < seqs)
                def _():
                    hop(True, t, z - t, i - t).start()

            @pl.when(live & (z + t < seqs))
            def _():
                hop(False, t, z + t, i - t).wait_recv()

                @pl.when(z > 0)
                def _():
                    hop(False, t, z + t, i - t).start()

        @pl.when(i < KVH // 2)
        def _():
            q_out(2 * i)
            q_out(2 * i + 1)

        @pl.when(i == min(2, seqs - 1))
        def _():
            prepare()

        @pl.when(i >= seqs - 1)
        def _():
            h = i - (seqs - 1)
            q_all(h).wait_recv()
            q_local(h).wait()
            attend(h)
            for d in peers:
                remote(
                    ob.at[h, slab_of(d)], home.at[slab_of(me), cols(h, wide)],
                    o_send.at[h], o_recv.at[h], (d, z),
                ).start()
            o_local(h).start()

    meta_all().wait_send()
    for k, p in enumerate(planes, 1):
        meta_hop(k, p, z).wait_send()

    @pl.loop(0, KVH)
    def _(h):
        kv_all(h).wait_send()
        q_all(h).wait_send()
        for t in range(seqs - 1):

            @pl.when((z >= t) & (z + 1 < seqs))
            def _():
                hop(True, t, z - t, h).wait_send()

            @pl.when((z + t < seqs) & (z > 0))
            def _():
                hop(False, t, z + t, h).wait_send()

        o_all(h).wait_send()
        o_all(h).wait_recv()
        o_local(h).wait()


def per_device(queries, keys, values, plan, segment_ids):
    rows = queries.shape[0]
    seqs = lax.axis_size("seq")
    dps = lax.axis_size("dp")
    group = rows * seqs
    share = rows // (seqs * dps)
    chunk = rows // seqs
    per_kv = H // KVH
    exponents = np.arange(HD // 2, dtype=np.float32)
    freqs = np.float32(theta_base) ** (np.float32(-2.0) * exponents / np.float32(HD))
    freqs = jnp.asarray(np.broadcast_to(np.concatenate([freqs, freqs])[None, :], (8, HD)))
    anywhere = pl.BlockSpec(memory_space=pl.ANY)
    inside = pl.BlockSpec(memory_space=pltpu.VMEM)
    dma = pltpu.SemaphoreType.DMA
    bf16, f32 = jnp.bfloat16, jnp.float32
    home, onehot = pl.pallas_call(
        functools.partial(travel, seqs, dps),
        in_specs=[anywhere, inside, inside, inside, inside, inside],
        out_specs=(anywhere, inside),
        out_shape=(
            jax.ShapeDtypeStruct(queries.shape, bf16),
            jax.ShapeDtypeStruct((rows, rows), bf16),
        ),
        scratch_shapes=[
            pltpu.VMEM((KVH, rows, per_kv * HD), bf16),
            pltpu.VMEM((KVH, rows, 2 * HD), bf16),
            pltpu.VMEM((rows, META), bf16),
            pltpu.VMEM((KVH, rows, per_kv * HD), bf16),
            pltpu.VMEM((seqs, KVH, rows, 2 * HD), bf16),
            pltpu.VMEM((seqs, rows + 16, META), bf16),
            pltpu.VMEM((KVH, rows, per_kv * HD), bf16),
            pltpu.VMEM((group, HD), bf16),
            pltpu.VMEM((group, HD), bf16),
            pltpu.VMEM((group, META), bf16),
            pltpu.VMEM((rows, HD), f32),
            pltpu.VMEM((rows, HD), f32),
            pltpu.VMEM((seqs, rows, HD), f32),
            pltpu.VMEM((seqs, rows, HD), f32),
            pltpu.VMEM((rows, group), f32),
            pltpu.VMEM((rows, per_kv * HD), bf16),
            dma((KVH,)), dma((KVH,)), dma((KVH,)),
            dma((KVH,)), dma((KVH,)), dma((KVH,)),
            dma((KVH,)), dma((KVH,)), dma((KVH,)), dma((KVH,)),
            dma, dma, dma, dma((seqs,)), dma((seqs,)),
            dma((2 * seqs, KVH)), dma((seqs, KVH)),
        ],
        compiler_params=pltpu.CompilerParams(
            collective_id=0, has_side_effects=True, vmem_limit_bytes=56 * 1024 * 1024
        ),
    )(queries, keys, values, plan[None, :], segment_ids[None, :], freqs)
    block = pl.BlockSpec((rows, per_kv * HD), lambda h: (0, h))
    return pl.pallas_call(
        restore,
        grid=(KVH,),
        in_specs=[pl.BlockSpec((rows, rows), lambda h: (0, 0)), block],
        out_specs=block,
        out_shape=jax.ShapeDtypeStruct(queries.shape, bf16),
    )(onehot, home)


def solution(mesh):
    return jax.shard_map(
        per_device,
        mesh=mesh,
        in_specs=(
            P(("dp", "seq"), None),
            P(("dp", "seq"), None),
            P(("dp", "seq"), None),
            P(("dp", "seq")),
            P(("dp", "seq")),
        ),
        out_specs=P(("dp", "seq"), None),
        check_vma=False,
    )
```
